32 devices in a mesh: fine: 8 (over y, x, core), coarse: 4 (over z).
Axes of the slice: x: 2, y: 2, z: 4, core: 2. Of those that a mesh axis runs over, the one named last changes fastest.
Arguments:
- force: float32 [3, 131072], P(None, ('fine', 'coarse')), may hold values from -6 to 6
- inv_diag: float32 [3, 131072], P(None, ('fine', 'coarse')), may hold values from 0.01 to 0.03
- k_ref: float32 [24, 24], replicated
- coefs: float32 [65536], P(('fine', 'coarse')), may hold values from 0.5 to 2
- conn: int32 [8, 65536], P(None, ('fine', 'coarse')), may hold values from 0 to 5119
- felem: int32 [24576], P(('fine', 'coarse')), may hold values from 0 to 2047
- weights: float32 [8, 8, 24576], P(None, None, ('fine', 'coarse')), may hold values from -0.6 to 0.6
- counts: int32 [32, 32], P(('fine', 'coarse')), may hold values from 1 to 24, as said below
- celem: int32 [32, 768], P(('fine', 'coarse')), may hold values from 0 to 127
Outputs:
- smoothed: float32 [3, 131072], P(None, ('fine', 'coarse'))
- coarse_load: float32 [24, 4096], P(None, ('fine', 'coarse'))
The draws below stay inside these ranges and needn't reach their ends.
Inputs may be any that keep to these rules, and one draw needn't show every extreme that they name: `counts`: in every draw one owner receives 24 used slots from every partition; every count is at least 1.
All inputs are finite; a program needn't handle non-finite values.
Results may differ from the reference program's by a relative error of at most 0.0003.
Values sent between devices are 32-bit elements; how exact they have to be, the bound alone decides.
A program may use at most 128 MiB of HBM per device.

```python
import math
import jax
import jax.numpy as jnp
from jax import lax

NODE_DEV = 4096
ELEM_DEV = 2048
BAND = 512
CAP = 24
CE_DEV = 128
OWNERS = 32
NODES = 131072
ELEMS = 65536
SLOTS = 24576
CE_ALL = 4096


def draw_k_ref(key, part):
    first = jax.random.fold_in(key, 11)
    second = jax.random.fold_in(key, 12)
    raw = jax.random.uniform(first, (24, 24), jnp.float32, -0.5, 0.5)
    sym = (raw + raw.T) * 0.5
    off = sym * (1.0 - jnp.eye(24, dtype=jnp.float32))
    extra = jax.random.uniform(second, (24,), jnp.float32, 0.5, 1.5)
    return off + jnp.diag(jnp.sum(jnp.abs(off), axis=1) + extra)


def draw_counts(key, part):
    first = jax.random.fold_in(key, 21)
    second = jax.random.fold_in(key, 22)
    third = jax.random.fold_in(key, 23)
    level = jax.random.randint(first, (OWNERS,), CAP // 2, CAP + 1)
    lower = jnp.maximum(level * 3 // 4, 1)
    drawn = jax.random.randint(second, (OWNERS, OWNERS), lower[None, :], level[None, :] + 1)
    busiest = jax.random.randint(third, (), 0, OWNERS)
    column = jnp.arange(OWNERS, dtype=jnp.int32)[None, :]
    return jnp.where(column == busiest, CAP, drawn).astype(jnp.int32)


def place_ends(array, stream_key, low, high):
    index_at = [jax.random.randint(jax.random.fold_in(stream_key, axis), (), 0, length) for axis, length in enumerate(array.shape)]
    main_axis = array.shape.index(max(array.shape))
    next_to = index_at[:main_axis] + [(index_at[main_axis] + 1) % array.shape[main_axis]] + index_at[main_axis + 1:]
    return array.at[tuple(index_at)].set(low).at[tuple(next_to)].set(high)


def levels(rng, shape, pieces, smallest, largest):
    def one(position, parts):
        steps = jax.random.uniform(jax.random.fold_in(jax.random.fold_in(rng, 6), position), (parts,), jnp.float32, smallest / len(pieces), largest / len(pieces))
        return jnp.repeat(jnp.exp(steps), shape[position] // parts).reshape((-1,) + (1,) * (len(shape) - position - 1))

    factor_of = one(*pieces[0])
    for cut in pieces[1:]:
        factor_of = factor_of * one(*cut)
    return factor_of


def centred(own_key, dims, width, most, cuts=(), kind=jnp.bfloat16):
    level = levels(own_key, dims, cuts, -0.22, 0.18) if cuts else 1.0
    entries = jax.random.normal(own_key, dims, jnp.float32) * width * level
    return jnp.minimum(jnp.maximum(entries, -most), most).astype(kind)


def setup_inputs(seed: int = 0) -> dict:
    streams_of = jax.random.split(jax.random.key(seed), 10)
    return {
        "force": centred(streams_of[0], (3, NODES), 1.0, 6.0, ((1, 32),), jnp.float32),
        "inv_diag": jnp.clip(jnp.exp(math.log(0.03) - 1.0986123 * jax.random.uniform(streams_of[1], (3, NODES), jnp.float32) ** levels(streams_of[1], (3, NODES), ((1, 32),), -0.2, 0.2)), 0.01, 0.03),
        "k_ref": draw_k_ref(jax.random.fold_in(streams_of[9], 71), 0),
        "coefs": jnp.clip(jnp.exp(math.log(2.0) - 1.3862944 * jax.random.uniform(streams_of[3], (ELEMS,), jnp.float32) ** levels(streams_of[3], (ELEMS,), ((0, 32),), -0.2, 0.2)), 0.5, 2.0),
        "conn": place_ends(jax.random.randint(streams_of[4], (8, ELEMS), 0, NODE_DEV + 2 * BAND), jax.random.fold_in(streams_of[4], 1), 0, (NODE_DEV + 2 * BAND) - 1).astype(jnp.int32),
        "felem": place_ends(jax.random.randint(streams_of[5], (SLOTS,), 0, ELEM_DEV), jax.random.fold_in(streams_of[5], 1), 0, ELEM_DEV - 1).astype(jnp.int32),
        "weights": centred(streams_of[6], (8, 8, SLOTS), 0.1, 0.6, ((2, 32),), jnp.float32),
        "counts": draw_counts(jax.random.fold_in(streams_of[9], 71), 0),
        "celem": place_ends(jax.random.randint(streams_of[8], (OWNERS, OWNERS * CAP), 0, CE_DEV), jax.random.fold_in(streams_of[8], 1), 0, CE_DEV - 1).astype(jnp.int32),
    }


LOW_END = 0.3
HIGH_END = 2.5


def apply_operator(field, k_ref, coefs, index):
    padded = jnp.pad(field, ((0, 0), (BAND, BAND)))
    local = padded[:, index].reshape(24, -1)
    product = jnp.dot(k_ref, local, precision=lax.Precision.HIGHEST, preferred_element_type=jnp.float32) * coefs[None, :]
    summed = jnp.zeros(padded.shape, jnp.float32).at[:, index].add(product.reshape(3, 8, -1))
    return summed[:, BAND:-BAND]


def reference(force, inv_diag, k_ref, coefs, conn, felem, weights, counts, celem):
    offset = (jnp.arange(ELEMS, dtype=jnp.int32) // ELEM_DEV) * NODE_DEV
    index = conn + offset[None, :]
    theta = (HIGH_END + LOW_END) / 2.0
    delta = (HIGH_END - LOW_END) / 2.0
    sigma = theta / delta
    rho = 1.0 / sigma
    solution = jnp.zeros_like(force)
    resid = force
    direction = inv_diag * resid / theta
    for sweep in range(3):
        solution = solution + direction
        resid = resid - apply_operator(direction, k_ref, coefs, index)
        if sweep < 2:
            rho_new = 1.0 / (2.0 * sigma - rho)
            direction = rho_new * rho * direction + (2.0 * rho_new / delta) * inv_diag * resid
            rho = rho_new
    padded_r = jnp.pad(resid, ((0, 0), (BAND, BAND)))
    per_src = OWNERS * CAP
    felem_blocks = felem.reshape(OWNERS, per_src)
    weight_blocks = jnp.transpose(weights.reshape(8, 8, OWNERS, per_src), (2, 0, 1, 3))
    slot_iota = jnp.arange(per_src, dtype=jnp.int32)

    def one_source(packed):
        source, fine_ids, block_w, count_row = packed
        elem_ids = fine_ids + source * ELEM_DEV
        node_ids = conn[:, elem_ids] + source * NODE_DEV
        values = padded_r[:, node_ids]
        contrib = jnp.einsum("ijs,cjs->cis", block_w, values, precision=lax.Precision.HIGHEST)
        live = (slot_iota % CAP) < count_row[slot_iota // CAP]
        return (contrib * live[None, None, :].astype(jnp.float32)).reshape(24, per_src)

    sources = jnp.arange(OWNERS, dtype=jnp.int32)
    contribs = lax.map(one_source, (sources, felem_blocks, weight_blocks, counts))
    data = jnp.transpose(contribs.reshape(OWNERS, 24, OWNERS, CAP), (0, 2, 3, 1)).reshape(-1, 24)
    owner_ids = jnp.transpose(celem.reshape(OWNERS, OWNERS, CAP), (1, 0, 2))
    owner_ids = owner_ids + (jnp.arange(OWNERS, dtype=jnp.int32) * CE_DEV)[None, :, None]
    load = jax.ops.segment_sum(data, owner_ids.reshape(-1), num_segments=CE_ALL)
    return solution, load.T
```

```python
import functools

import jax
import jax.numpy as jnp
from jax import lax
from jax.experimental import pallas as pl
from jax.experimental.pallas import tpu as pltpu
from jax.sharding import PartitionSpec as P

BAND = 512
CAP = 24
CE_DEV = 128
LOW_END = 0.3
HIGH_END = 2.5
SWEEPS = 3
LANES = 128
ROW = 256
SPACE = 32
GROUP = 16
TILES = 4

THETA = (HIGH_END + LOW_END) / 2.0
DELTA = (HIGH_END - LOW_END) / 2.0
SIGMA = THETA / DELTA


def schedule():
    rho = 1.0 / SIGMA
    steps = []
    for _ in range(SWEEPS - 1):
        rho_new = 1.0 / (2.0 * SIGMA - rho)
        steps.append((rho_new * rho, 2.0 * rho_new / DELTA))
        rho = rho_new
    return steps + [(0.0, 0.0)]


def split(value):
    high = value.astype(jnp.bfloat16).astype(jnp.float32)
    return (high, value - high)


def pick(row, index):
    table = jnp.broadcast_to(row, index.shape)
    return jnp.take_along_axis(table, index, axis=1, mode="promise_in_bounds")


def spread(tiles, lane, local):
    first, at = divmod(local * CAP, LANES)
    out = None
    for c, row in enumerate(tiles):
        piece = pltpu.roll(row[first], (c * SPACE - at) % LANES, axis=1)
        left = LANES - at
        if left < CAP:
            rest = pltpu.roll(row[first + 1], (c * SPACE + left) % LANES, axis=1)
            piece = jnp.where(lane < c * SPACE + left, piece, rest)
        out = piece if c == 0 else jnp.where(lane < c * SPACE, out, piece)
    return out


def kernel(
    sizes, force, inv_diag, k_ref, coefs, conn, felem, weights, counts, celem,
    smoothed, load,
    direction, resid, scale, total, part, local, onehot, slot_node, values, contrib,
    sent, selector, arrived, stacked, snd, rcv,
    snd_sem, rcv_sem, out_sem, in_sem, own_sem,
):
    fine, coarse = sizes
    devices = fine * coarse
    me = lax.axis_index("fine") * coarse + lax.axis_index("coarse")
    nodes = force.shape[1]
    owned = nodes // ROW
    edge = BAND // ROW
    rows = owned + 2 * edge
    stride = total.shape[0] // 3
    elems = conn.shape[1]
    slots = felem.shape[1]
    window = 2 * edge

    def place(index):
        return (index // coarse, lax.rem(index, coarse))

    barrier = pltpu.get_barrier_semaphore()

    @pl.loop(1, devices)
    def _(step):
        pl.semaphore_signal(
            barrier, inc=1, device_id=place(lax.rem(me + step, devices)),
            device_id_type=pl.DeviceIdType.MESH,
        )

    resid[...] = jnp.zeros_like(resid)
    scale[...] = jnp.zeros_like(scale)
    for c in range(3):
        for h in range(owned):
            at = c * stride + edge + h
            resid[at : at + 1, :] = force[c : c + 1, h * ROW : (h + 1) * ROW]
            scale[at : at + 1, :] = inv_diag[c : c + 1, h * ROW : (h + 1) * ROW]
    for d, begin in enumerate((edge, owned)):
        for a, field in enumerate((resid, scale)):
            for c in range(3):
                at = c * stride + begin
                to = (a * 3 + c) * edge
                snd[0, d, to : to + edge, :] = field[at : at + edge, :]

    @pl.loop(0, 8)
    def _(j):
        low = jnp.bitwise_and(conn[pl.ds(j, 1), :], ROW - 1)
        hit = lax.broadcasted_iota(jnp.int32, (ROW, elems), 0) == low
        onehot[j] = jnp.where(hit, 1.0, 0.0).astype(jnp.bfloat16)

    @pl.loop(0, slots // LANES)
    def _(tile):
        at = pl.multiple_of(tile * LANES, LANES)
        element = jnp.broadcast_to(felem[:, pl.ds(at, LANES)], (8, LANES))
        low = jnp.bitwise_and(element, LANES - 1)
        high = lax.shift_right_logical(element, 7)
        found = jnp.zeros((8, LANES), jnp.int32)
        for t in range(elems // LANES):
            got = jnp.take_along_axis(
                conn[:, t * LANES : (t + 1) * LANES], low, axis=1, mode="promise_in_bounds"
            )
            found = jnp.where(high == t, got, found)
        slot_node[:, pl.ds(at, LANES)] = found

    lane = lax.broadcasted_iota(jnp.int32, (8, LANES), 1)
    coarse_iota = lax.broadcasted_iota(jnp.int32, (CE_DEV, LANES), 0)
    group_tiles = GROUP * CAP // LANES

    @pl.loop(0, devices // GROUP)
    def _(group):
        base = group * (GROUP * CAP)
        ids = [
            jnp.broadcast_to(
                celem[:, pl.ds(pl.multiple_of(base + t * LANES, LANES), LANES)], (8, LANES)
            )
            for t in range(group_tiles)
        ]
        for o in range(GROUP):
            owner = spread([ids, ids, ids], lane, o)
            hit = coarse_iota == owner[0:1, :]
            at = pl.multiple_of((group * GROUP + o) * LANES, LANES)
            selector[:, pl.ds(at, LANES)] = jnp.where(hit, 1.0, 0.0).astype(jnp.bfloat16)

    pl.semaphore_wait(barrier, devices - 1)

    lower, upper = (place(lax.rem(me + devices - 1, devices)), place(lax.rem(me + 1, devices)))

    def edge_copy(phase, d, target):
        return pltpu.make_async_remote_copy(
            src_ref=snd.at[phase, d],
            dst_ref=rcv.at[phase, d],
            send_sem=snd_sem.at[phase, d],
            recv_sem=rcv_sem.at[phase, d],
            device_id=target,
            device_id_type=pl.DeviceIdType.MESH,
        )

    def exchange(phase):
        down, up = edge_copy(phase, 0, lower), edge_copy(phase, 1, upper)

        @pl.when(me > 0)
        def _():
            down.start()

        @pl.when(me < devices - 1)
        def _():
            up.start()

        @pl.when(me > 0)
        def _():
            up.wait_recv()
            down.wait_send()

        @pl.when(me < devices - 1)
        def _():
            down.wait_recv()
            up.wait_send()

    exchange(0)

    @pl.when(me > 0)
    def _():
        for a, field in enumerate((resid, scale)):
            for c in range(3):
                at, to = (c * stride, (a * 3 + c) * edge)
                field[at : at + edge, :] = rcv[0, 1, to : to + edge, :]

    @pl.when(me < devices - 1)
    def _():
        for a, field in enumerate((resid, scale)):
            for c in range(3):
                at, to = (c * stride + edge + owned, (a * 3 + c) * edge)
                field[at : at + edge, :] = rcv[0, 0, to : to + edge, :]

    direction[...] = scale[...] * resid[...] / THETA
    total[...] = jnp.zeros_like(total)

    def gather(field, index, count):
        low = [jnp.bitwise_and(i, LANES - 1) for i in index]
        high = [lax.shift_right_logical(i, 7) for i in index]
        out = [[jnp.zeros((8, LANES), jnp.float32) for _ in range(count)] for _ in range(3)]
        for h in range(rows * ROW // LANES):
            at, side = divmod(h, ROW // LANES)
            here = [i == h for i in high]
            for c in range(3):
                r = c * stride + at
                row = field[r : r + 1, side * LANES : (side + 1) * LANES]
                for t in range(count):
                    out[c][t] = jnp.where(here[t], pick(row, low[t]), out[c][t])
        return out

    row_iota = lax.broadcasted_iota(jnp.int32, (stride, elems), 0)
    steps = schedule()

    @pl.loop(0, SWEEPS)
    def _(sweep):
        total[...] += direction[...]

        @pl.loop(0, elems // (LANES * TILES))
        def _(chunk):
            starts = [pl.multiple_of((chunk * TILES + t) * LANES, LANES) for t in range(TILES)]
            index = [conn[:, pl.ds(s, LANES)] for s in starts]
            got = gather(direction, index, TILES)
            for c in range(3):
                for t in range(TILES):
                    local[c * 8 : (c + 1) * 8, pl.ds(starts[t], LANES)] = got[c][t]

        product = (
            jnp.dot(
                k_ref[...], local[...], precision=lax.Precision.HIGHEST,
                preferred_element_type=jnp.float32,
            )
            * coefs[...]
        )
        local[...] = product
        part[...] = jnp.zeros_like(part)

        @pl.loop(0, 8)
        def _(j):
            high = lax.shift_right_logical(conn[pl.ds(j, 1), :], 8)
            hit = row_iota == high
            halves = [split(local[pl.ds(c * 8 + j, 1), :]) for c in range(3)]
            left = jnp.concatenate(
                [jnp.where(hit, halves[c][s], 0.0) for s in range(2) for c in range(3)], axis=0
            ).astype(jnp.bfloat16)
            part[...] += lax.dot_general(
                left, onehot[j], (((1,), (1,)), ((), ())), preferred_element_type=jnp.float32
            )

        both = part[: 3 * stride, :] + part[3 * stride :, :]
        part[: 3 * stride, :] = both
        for d, begin in enumerate((0, owned)):
            for c in range(3):
                at = c * stride + begin
                snd[sweep + 1, d, c * window : (c + 1) * window, :] = part[at : at + window, :]
        exchange(sweep + 1)

        @pl.when(me > 0)
        def _():
            for c in range(3):
                part[c * stride : c * stride + window, :] += rcv[
                    sweep + 1, 1, c * window : (c + 1) * window, :
                ]

        @pl.when(me == 0)
        def _():
            for c in range(3):
                part[c * stride : c * stride + edge, :] = jnp.zeros((edge, ROW), jnp.float32)

        @pl.when(me < devices - 1)
        def _():
            for c in range(3):
                at = c * stride + owned
                part[at : at + window, :] += rcv[sweep + 1, 0, c * window : (c + 1) * window, :]

        @pl.when(me == devices - 1)
        def _():
            for c in range(3):
                at = c * stride + edge + owned
                part[at : at + edge, :] = jnp.zeros((edge, ROW), jnp.float32)

        new = resid[...] - part[: 3 * stride, :]
        resid[...] = new
        keep = jnp.where(sweep == 0, steps[0][0], steps[1][0])
        add = jnp.where(sweep == 0, steps[0][1], steps[1][1])
        direction[...] = keep * direction[...] + add * scale[...] * new

    @pl.loop(0, slots // LANES)
    def _(tile):
        at = pl.multiple_of(tile * LANES, LANES)
        got = gather(resid, [slot_node[:, pl.ds(at, LANES)]], 1)
        for c in range(3):
            values[c * 8 : (c + 1) * 8, :] = got[c][0]
        for c in range(3):
            acc = jnp.zeros((8, LANES), jnp.float32)
            for j in range(8):
                acc = acc + weights[:, j, pl.ds(at, LANES)] * values[c * 8 + j : c * 8 + j + 1, :]
            contrib[c * 8 : (c + 1) * 8, pl.ds(at, LANES)] = acc

    lane_slot = jnp.bitwise_and(lane, SPACE - 1)

    @pl.loop(0, devices // GROUP)
    def _(group):
        base = group * (GROUP * CAP)
        tiles = [
            [
                contrib[
                    c * 8 : (c + 1) * 8,
                    pl.ds(pl.multiple_of(base + t * LANES, LANES), LANES),
                ]
                for t in range(group_tiles)
            ]
            for c in range(3)
        ]
        for o in range(GROUP):
            owner = group * GROUP + o
            live = (lane_slot < counts[0, owner]) & (lane < 3 * SPACE)
            sent[owner] = jnp.where(live, spread(tiles, lane, o), 0.0)

    def slot_copy(target):
        return pltpu.make_async_remote_copy(
            src_ref=sent.at[target],
            dst_ref=arrived.at[me],
            send_sem=out_sem.at[target],
            recv_sem=in_sem.at[me],
            device_id=place(target),
            device_id_type=pl.DeviceIdType.MESH,
        )

    def slot_arrival(source):
        return pltpu.make_async_remote_copy(
            src_ref=sent.at[source],
            dst_ref=arrived.at[source],
            send_sem=out_sem.at[source],
            recv_sem=in_sem.at[source],
            device_id=place(source),
            device_id_type=pl.DeviceIdType.MESH,
        )

    @pl.loop(1, devices)
    def _(step):
        slot_copy(lax.rem(me + step, devices)).start()

    own = pltpu.make_async_copy(sent.at[me], arrived.at[me], own_sem)
    own.start()

    for c in range(3):
        for h in range(owned):
            at = c * stride + edge + h
            smoothed[c : c + 1, h * ROW : (h + 1) * ROW] = total[at : at + 1, :]

    own.wait()

    @pl.loop(1, devices)
    def _(step):
        slot_arrival(lax.rem(me + step, devices)).wait_recv()

    @pl.loop(0, devices)
    def _(source):
        got = arrived[source]
        pieces = [
            split(jnp.where((lane >= c * SPACE) & (lane < (c + 1) * SPACE), got, 0.0))
            for c in range(3)
        ]
        stacked[:, pl.ds(pl.multiple_of(source * LANES, LANES), LANES)] = jnp.concatenate(
            [pieces[c][s] for s in range(2) for c in range(3)], axis=0
        ).astype(jnp.bfloat16)

    sums = lax.dot_general(
        stacked[...], selector[...], (((1,), (1,)), ((), ())), preferred_element_type=jnp.float32
    )
    load[...] = sums[:24, :] + sums[24:, :]

    @pl.loop(1, devices)
    def _(step):
        slot_copy(lax.rem(me + step, devices)).wait_send()


def on_device(sizes, force, inv_diag, k_ref, coefs, conn, felem, weights, counts, celem):
    devices = sizes[0] * sizes[1]
    nodes = force.shape[1]
    elems = conn.shape[1]
    slots = felem.shape[0]
    rows = (nodes + 2 * BAND) // ROW
    stride = -(-rows // 8) * 8
    edge_rows = 6 * BAND // ROW
    field = pltpu.VMEM((3 * stride, ROW), jnp.float32)
    edges = pltpu.VMEM((SWEEPS + 1, 2, edge_rows, ROW), jnp.float32)
    vmem = pl.BlockSpec(memory_space=pltpu.VMEM)
    smem = pl.BlockSpec(memory_space=pltpu.SMEM)
    return pl.pallas_call(
        functools.partial(kernel, sizes),
        out_shape=(
            jax.ShapeDtypeStruct((3, nodes), jnp.float32),
            jax.ShapeDtypeStruct((24, CE_DEV), jnp.float32),
        ),
        in_specs=[vmem] * 7 + [smem, vmem],
        out_specs=(vmem, vmem),
        scratch_shapes=[
            field,
            field,
            field,
            field,
            pltpu.VMEM((6 * stride, ROW), jnp.float32),
            pltpu.VMEM((24, elems), jnp.float32),
            pltpu.VMEM((8, ROW, elems), jnp.bfloat16),
            pltpu.VMEM((8, slots), jnp.int32),
            pltpu.VMEM((24, LANES), jnp.float32),
            pltpu.VMEM((24, slots), jnp.float32),
            pltpu.VMEM((devices, 8, LANES), jnp.float32),
            pltpu.VMEM((CE_DEV, devices * LANES), jnp.bfloat16),
            pltpu.VMEM((devices, 8, LANES), jnp.float32),
            pltpu.VMEM((48, devices * LANES), jnp.bfloat16),
            edges,
            edges,
            pltpu.SemaphoreType.DMA((SWEEPS + 1, 2)),
            pltpu.SemaphoreType.DMA((SWEEPS + 1, 2)),
            pltpu.SemaphoreType.DMA((devices,)),
            pltpu.SemaphoreType.DMA((devices,)),
            pltpu.SemaphoreType.DMA,
        ],
        compiler_params=pltpu.CompilerParams(
            collective_id=0, has_side_effects=True, vmem_limit_bytes=48 * 1024 * 1024
        ),
    )(force, inv_diag, k_ref, coefs[None, :], conn, felem[None, :], weights, counts, celem)


def solution(mesh):
    both = ("fine", "coarse")
    placed = (
        P(None, both),
        P(None, both),
        P(),
        P(both),
        P(None, both),
        P(both),
        P(None, None, both),
        P(both, None),
        P(both, None),
    )
    sizes = (mesh.shape["fine"], mesh.shape["coarse"])
    return jax.shard_map(
        functools.partial(on_device, sizes),
        mesh=mesh,
        in_specs=placed,
        out_specs=(P(None, both), P(None, both)),
        check_vma=False,
    )
```

```python
import functools

import jax
import jax.numpy as jnp
from jax import lax
from jax.experimental import pallas as pl
from jax.experimental.pallas import tpu as pltpu
from jax.sharding import PartitionSpec as P

BAND = 512
CAP = 24
CE_DEV = 128
LOW_END = 0.3
HIGH_END = 2.5
SWEEPS = 3
LANES = 128
ROW = 256
SPACE = 32
GROUP = 16
TILES = 2

THETA = (HIGH_END + LOW_END) / 2.0
DELTA = (HIGH_END - LOW_END) / 2.0
SIGMA = THETA / DELTA


def schedule():
    rho = 1.0 / SIGMA
    steps = []
    for _ in range(SWEEPS - 1):
        rho_new = 1.0 / (2.0 * SIGMA - rho)
        steps.append((rho_new * rho, 2.0 * rho_new / DELTA))
        rho = rho_new
    return steps + [(0.0, 0.0)]


def split(value):
    high = value.astype(jnp.bfloat16).astype(jnp.float32)
    return (high, value - high)


def pick(row, index):
    table = jnp.broadcast_to(row, index.shape)
    return jnp.take_along_axis(table, index, axis=1, mode="promise_in_bounds")


def spread(tiles, lane, local):
    first, at = divmod(local * CAP, LANES)
    out = None
    for c, row in enumerate(tiles):
        piece = pltpu.roll(row[first], (c * SPACE - at) % LANES, axis=1)
        left = LANES - at
        if left < CAP:
            rest = pltpu.roll(row[first + 1], (c * SPACE + left) % LANES, axis=1)
            piece = jnp.where(lane < c * SPACE + left, piece, rest)
        out = piece if c == 0 else jnp.where(lane < c * SPACE, out, piece)
    return out


def kernel(
    sizes, force_in, inv_diag_in, k_ref_in, coefs_in, conn_in, felem_in, weights_in, counts,
    celem_in, smoothed, load,
    force, inv_diag, k_ref, coefs, conn, felem, weights, celem,
    direction, resid, scale, total, part, local, onehot, slot_node, values, contrib,
    sent, selector, arrived, stacked, snd, rcv,
    snd_sem, rcv_sem, out_sem, in_sem, own_sem, load_sem,
):
    fine, coarse = sizes
    devices = fine * coarse
    me = lax.axis_index("fine") * coarse + lax.axis_index("coarse")
    nodes = force.shape[1]
    owned = nodes // ROW
    edge = BAND // ROW
    rows = owned + 2 * edge
    stride = total.shape[0] // 3
    elems = conn.shape[1]
    slots = felem.shape[1]
    window = 2 * edge

    def place(index):
        return (index // coarse, lax.rem(index, coarse))

    pairs = [
        (force_in, force), (inv_diag_in, inv_diag), (conn_in, conn), (felem_in, felem.at[0]),
        (celem_in, celem), (k_ref_in, k_ref), (coefs_in, coefs.at[0]), (weights_in, weights),
    ]
    loads = [pltpu.make_async_copy(a, b, load_sem.at[n]) for n, (a, b) in enumerate(pairs)]
    for copy in loads:
        copy.start()

    barrier = pltpu.get_barrier_semaphore()

    @pl.loop(1, devices)
    def _(step):
        pl.semaphore_signal(
            barrier, inc=1, device_id=place(lax.rem(me + step, devices)),
            device_id_type=pl.DeviceIdType.MESH,
        )

    resid[...] = jnp.zeros_like(resid)
    scale[...] = jnp.zeros_like(scale)
    loads[0].wait()
    loads[1].wait()
    for c in range(3):
        for h in range(owned):
            at = c * stride + edge + h
            resid[at : at + 1, :] = force[c : c + 1, h * ROW : (h + 1) * ROW]
            scale[at : at + 1, :] = inv_diag[c : c + 1, h * ROW : (h + 1) * ROW]
    for d, begin in enumerate((edge, owned)):
        for a, field in enumerate((resid, scale)):
            for c in range(3):
                at = c * stride + begin
                to = (a * 3 + c) * edge
                snd[0, d, to : to + edge, :] = field[at : at + edge, :]

    for copy in loads[2:5]:
        copy.wait()

    @pl.loop(0, 8)
    def _(j):
        low = jnp.bitwise_and(conn[pl.ds(j, 1), :], ROW - 1)
        hit = lax.broadcasted_iota(jnp.int32, (ROW, elems), 0) == low
        onehot[j] = jnp.where(hit, 1.0, 0.0).astype(jnp.bfloat16)

    @pl.loop(0, slots // LANES)
    def _(tile):
        at = pl.multiple_of(tile * LANES, LANES)
        element = jnp.broadcast_to(felem[:, pl.ds(at, LANES)], (8, LANES))
        low = jnp.bitwise_and(element, LANES - 1)
        high = lax.shift_right_logical(element, 7)
        found = jnp.zeros((8, LANES), jnp.int32)
        for t in range(elems // LANES):
            got = jnp.take_along_axis(
                conn[:, t * LANES : (t + 1) * LANES], low, axis=1, mode="promise_in_bounds"
            )
            found = jnp.where(high == t, got, found)
        slot_node[:, pl.ds(at, LANES)] = found

    lane = lax.broadcasted_iota(jnp.int32, (8, LANES), 1)
    coarse_iota = lax.broadcasted_iota(jnp.int32, (CE_DEV, LANES), 0)
    group_tiles = GROUP * CAP // LANES

    @pl.loop(0, devices // GROUP)
    def _(group):
        base = group * (GROUP * CAP)
        ids = [
            jnp.broadcast_to(
                celem[:, pl.ds(pl.multiple_of(base + t * LANES, LANES), LANES)], (8, LANES)
            )
            for t in range(group_tiles)
        ]
        for o in range(GROUP):
            owner = spread([ids, ids, ids], lane, o)
            hit = coarse_iota == owner[0:1, :]
            at = pl.multiple_of((group * GROUP + o) * LANES, LANES)
            selector[:, pl.ds(at, LANES)] = jnp.where(hit, 1.0, 0.0).astype(jnp.bfloat16)

    pl.semaphore_wait(barrier, devices - 1)

    lower, upper = (place(lax.rem(me + devices - 1, devices)), place(lax.rem(me + 1, devices)))

    def edge_copy(phase, d, target):
        return pltpu.make_async_remote_copy(
            src_ref=snd.at[phase, d],
            dst_ref=rcv.at[phase, d],
            send_sem=snd_sem.at[phase, d],
            recv_sem=rcv_sem.at[phase, d],
            device_id=target,
            device_id_type=pl.DeviceIdType.MESH,
        )

    def edge_start(phase):
        down, up = edge_copy(phase, 0, lower), edge_copy(phase, 1, upper)

        @pl.when(me > 0)
        def _():
            down.start()

        @pl.when(me < devices - 1)
        def _():
            up.start()

    def edge_wait(phase):
        down, up = edge_copy(phase, 0, lower), edge_copy(phase, 1, upper)

        @pl.when(me > 0)
        def _():
            up.wait_recv()
            down.wait_send()

        @pl.when(me < devices - 1)
        def _():
            down.wait_recv()
            up.wait_send()

    edge_start(0)
    for copy in loads[5:]:
        copy.wait()

    def fill_edges():
        @pl.when(me > 0)
        def _():
            for a, field in enumerate((resid, scale)):
                for c in range(3):
                    at, to = (c * stride, (a * 3 + c) * edge)
                    field[at : at + edge, :] = rcv[0, 1, to : to + edge, :]

        @pl.when(me < devices - 1)
        def _():
            for a, field in enumerate((resid, scale)):
                for c in range(3):
                    at, to = (c * stride + edge + owned, (a * 3 + c) * edge)
                    field[at : at + edge, :] = rcv[0, 0, to : to + edge, :]

        direction[...] = scale[...] * resid[...] / THETA

    def add_edges(phase, add):
        def from_side(d, begin):
            for c in range(3):
                at = slice(c * stride + begin, c * stride + begin + window)
                theirs = rcv[phase, d, c * window : (c + 1) * window, :]
                resid[at, :] -= theirs
                direction[at, :] -= add * scale[at, :] * theirs

        def clear(begin):
            for c in range(3):
                at = c * stride + begin
                resid[at : at + edge, :] = jnp.zeros((edge, ROW), jnp.float32)

        @pl.when(me > 0)
        def _():
            from_side(1, 0)

        @pl.when(me == 0)
        def _():
            clear(0)

        @pl.when(me < devices - 1)
        def _():
            from_side(0, owned)

        @pl.when(me == devices - 1)
        def _():
            clear(edge + owned)

    direction[...] = scale[...] * resid[...] / THETA
    total[...] = jnp.zeros_like(total)

    per_row = ROW // LANES
    inner = range(window * per_row, owned * per_row)
    outer = [h for h in range(rows * per_row) if h not in inner]

    def gather(field, index, hs, out):
        low = [jnp.bitwise_and(i, LANES - 1) for i in index]
        high = [lax.shift_right_logical(i, 7) for i in index]
        for h in hs:
            at, side = divmod(h, per_row)
            here = [i == h for i in high]
            for c in range(3):
                r = c * stride + at
                row = field[r : r + 1, side * LANES : (side + 1) * LANES]
                for t in range(len(index)):
                    out[c][t] = jnp.where(here[t], pick(row, low[t]), out[c][t])
        return out

    def gather_local(hs, first):
        @pl.loop(0, elems // (LANES * TILES))
        def _(chunk):
            starts = [pl.multiple_of((chunk * TILES + t) * LANES, LANES) for t in range(TILES)]
            index = [conn[:, pl.ds(s, LANES)] for s in starts]
            out = [
                [
                    jnp.zeros((8, LANES), jnp.float32)
                    if first
                    else local[c * 8 : (c + 1) * 8, pl.ds(starts[t], LANES)]
                    for t in range(TILES)
                ]
                for c in range(3)
            ]
            got = gather(direction, index, hs, out)
            for c in range(3):
                for t in range(TILES):
                    local[c * 8 : (c + 1) * 8, pl.ds(starts[t], LANES)] = got[c][t]

    row_iota = lax.broadcasted_iota(jnp.int32, (stride, elems), 0)
    steps = schedule()

    @pl.loop(0, SWEEPS)
    def _(sweep):
        gather_local(inner, True)
        edge_wait(sweep)

        @pl.when(sweep == 0)
        def _():
            fill_edges()

        @pl.when(sweep > 0)
        def _():
            add_edges(sweep, jnp.where(sweep == 1, steps[0][1], steps[1][1]))

        total[...] += direction[...]
        gather_local(outer, False)

        product = (
            jnp.dot(
                k_ref[...], local[...], precision=lax.Precision.HIGHEST,
                preferred_element_type=jnp.float32,
            )
            * coefs[...]
        )
        local[...] = product
        part[...] = jnp.zeros_like(part)

        @pl.loop(0, 8, unroll=True)
        def _(j):
            high = lax.shift_right_logical(conn[pl.ds(j, 1), :], 8)
            hit = row_iota == high
            halves = [split(local[pl.ds(c * 8 + j, 1), :]) for c in range(3)]
            left = jnp.concatenate(
                [jnp.where(hit, halves[c][s], 0.0) for s in range(2) for c in range(3)], axis=0
            ).astype(jnp.bfloat16)
            part[...] += lax.dot_general(
                left, onehot[j], (((1,), (1,)), ((), ())), preferred_element_type=jnp.float32
            )

        both = part[: 3 * stride, :] + part[3 * stride :, :]
        part[: 3 * stride, :] = both
        for d, begin in enumerate((0, owned)):
            for c in range(3):
                at = c * stride + begin
                snd[sweep + 1, d, c * window : (c + 1) * window, :] = part[at : at + window, :]
        edge_start(sweep + 1)
        new = resid[...] - part[: 3 * stride, :]
        resid[...] = new
        keep = jnp.where(sweep == 0, steps[0][0], steps[1][0])
        add = jnp.where(sweep == 0, steps[0][1], steps[1][1])
        direction[...] = keep * direction[...] + add * scale[...] * new

    @pl.loop(0, slots // LANES)
    def _(tile):
        at = pl.multiple_of(tile * LANES, LANES)
        begun = [[jnp.zeros((8, LANES), jnp.float32)] for _ in range(3)]
        got = gather(resid, [slot_node[:, pl.ds(at, LANES)]], inner, begun)
        for c in range(3):
            contrib[c * 8 : (c + 1) * 8, pl.ds(at, LANES)] = got[c][0]

    edge_wait(SWEEPS)
    add_edges(SWEEPS, 0.0)

    @pl.loop(0, slots // LANES)
    def _(tile):
        at = pl.multiple_of(tile * LANES, LANES)
        begun = [[contrib[c * 8 : (c + 1) * 8, pl.ds(at, LANES)]] for c in range(3)]
        got = gather(resid, [slot_node[:, pl.ds(at, LANES)]], outer, begun)
        for c in range(3):
            values[c * 8 : (c + 1) * 8, :] = got[c][0]
        for c in range(3):
            acc = jnp.zeros((8, LANES), jnp.float32)
            for j in range(8):
                acc = acc + weights[:, j, pl.ds(at, LANES)] * values[c * 8 + j : c * 8 + j + 1, :]
            contrib[c * 8 : (c + 1) * 8, pl.ds(at, LANES)] = acc

    lane_slot = jnp.bitwise_and(lane, SPACE - 1)

    @pl.loop(0, devices // GROUP)
    def _(group):
        base = group * (GROUP * CAP)
        tiles = [
            [
                contrib[
                    c * 8 : (c + 1) * 8,
                    pl.ds(pl.multiple_of(base + t * LANES, LANES), LANES),
                ]
                for t in range(group_tiles)
            ]
            for c in range(3)
        ]
        for o in range(GROUP):
            owner = group * GROUP + o
            live = (lane_slot < counts[0, owner]) & (lane < 3 * SPACE)
            sent[owner] = jnp.where(live, spread(tiles, lane, o), 0.0)

    def slot_copy(target):
        return pltpu.make_async_remote_copy(
            src_ref=sent.at[target],
            dst_ref=arrived.at[me],
            send_sem=out_sem.at[target],
            recv_sem=in_sem.at[me],
            device_id=place(target),
            device_id_type=pl.DeviceIdType.MESH,
        )

    def slot_arrival(source):
        return pltpu.make_async_remote_copy(
            src_ref=sent.at[source],
            dst_ref=arrived.at[source],
            send_sem=out_sem.at[source],
            recv_sem=in_sem.at[source],
            device_id=place(source),
            device_id_type=pl.DeviceIdType.MESH,
        )

    @pl.loop(1, devices)
    def _(step):
        slot_copy(lax.rem(me + step, devices)).start()

    own = pltpu.make_async_copy(sent.at[me], arrived.at[me], own_sem)
    own.start()

    for c in range(3):
        for h in range(owned):
            at = c * stride + edge + h
            smoothed[c : c + 1, h * ROW : (h + 1) * ROW] = total[at : at + 1, :]

    own.wait()

    @pl.loop(1, devices)
    def _(step):
        slot_arrival(lax.rem(me + step, devices)).wait_recv()

    @pl.loop(0, devices)
    def _(source):
        got = arrived[source]
        pieces = [
            split(jnp.where((lane >= c * SPACE) & (lane < (c + 1) * SPACE), got, 0.0))
            for c in range(3)
        ]
        stacked[:, pl.ds(pl.multiple_of(source * LANES, LANES), LANES)] = jnp.concatenate(
            [pieces[c][s] for s in range(2) for c in range(3)], axis=0
        ).astype(jnp.bfloat16)

    sums = lax.dot_general(
        stacked[...], selector[...], (((1,), (1,)), ((), ())), preferred_element_type=jnp.float32
    )
    load[...] = sums[:24, :] + sums[24:, :]

    @pl.loop(1, devices)
    def _(step):
        slot_copy(lax.rem(me + step, devices)).wait_send()


def on_device(sizes, force, inv_diag, k_ref, coefs, conn, felem, weights, counts, celem):
    devices = sizes[0] * sizes[1]
    nodes = force.shape[1]
    elems = conn.shape[1]
    slots = felem.shape[0]
    rows = (nodes + 2 * BAND) // ROW
    stride = -(-rows // 8) * 8
    edge_rows = 6 * BAND // ROW
    field = pltpu.VMEM((3 * stride, ROW), jnp.float32)
    edges = pltpu.VMEM((SWEEPS + 1, 2, edge_rows, ROW), jnp.float32)
    vmem = pl.BlockSpec(memory_space=pltpu.VMEM)
    hbm = pl.BlockSpec(memory_space=pltpu.HBM)
    smem = pl.BlockSpec(memory_space=pltpu.SMEM)
    return pl.pallas_call(
        functools.partial(kernel, sizes),
        out_shape=(
            jax.ShapeDtypeStruct((3, nodes), jnp.float32),
            jax.ShapeDtypeStruct((24, CE_DEV), jnp.float32),
        ),
        in_specs=[hbm] * 7 + [smem, hbm],
        out_specs=(vmem, vmem),
        scratch_shapes=[
            pltpu.VMEM((3, nodes), jnp.float32),
            pltpu.VMEM((3, nodes), jnp.float32),
            pltpu.VMEM((24, 24), jnp.float32),
            pltpu.VMEM((1, elems), jnp.float32),
            pltpu.VMEM((8, elems), jnp.int32),
            pltpu.VMEM((1, slots), jnp.int32),
            pltpu.VMEM((8, 8, slots), jnp.float32),
            pltpu.VMEM((1, slots), jnp.int32),
            field,
            field,
            field,
            field,
            pltpu.VMEM((6 * stride, ROW), jnp.float32),
            pltpu.VMEM((24, elems), jnp.float32),
            pltpu.VMEM((8, ROW, elems), jnp.bfloat16),
            pltpu.VMEM((8, slots), jnp.int32),
            pltpu.VMEM((24, LANES), jnp.float32),
            pltpu.VMEM((24, slots), jnp.float32),
            pltpu.VMEM((devices, 8, LANES), jnp.float32),
            pltpu.VMEM((CE_DEV, devices * LANES), jnp.bfloat16),
            pltpu.VMEM((devices, 8, LANES), jnp.float32),
            pltpu.VMEM((48, devices * LANES), jnp.bfloat16),
            edges,
            edges,
            pltpu.SemaphoreType.DMA((SWEEPS + 1, 2)),
            pltpu.SemaphoreType.DMA((SWEEPS + 1, 2)),
            pltpu.SemaphoreType.DMA((devices,)),
            pltpu.SemaphoreType.DMA((devices,)),
            pltpu.SemaphoreType.DMA,
            pltpu.SemaphoreType.DMA((8,)),
        ],
        compiler_params=pltpu.CompilerParams(
            collective_id=0, has_side_effects=True, vmem_limit_bytes=64 * 1024 * 1024
        ),
    )(force, inv_diag, k_ref, coefs, conn, felem, weights, counts, celem)


def solution(mesh):
    both = ("fine", "coarse")
    placed = (
        P(None, both),
        P(None, both),
        P(),
        P(both),
        P(None, both),
        P(both),
        P(None, None, both),
        P(both, None),
        P(both, None),
    )
    sizes = (mesh.shape["fine"], mesh.shape["coarse"])
    return jax.shard_map(
        functools.partial(on_device, sizes),
        mesh=mesh,
        in_specs=placed,
        out_specs=(P(None, both), P(None, both)),
        check_vma=False,
    )
```

```python
import functools

import jax
import jax.numpy as jnp
from jax import lax
from jax.experimental import pallas as pl
from jax.experimental.pallas import tpu as pltpu
from jax.sharding import PartitionSpec as P

BAND = 512
CAP = 24
CE_DEV = 128
LOW_END = 0.3
HIGH_END = 2.5
SWEEPS = 3
LANES = 128
ROW = 256
SPACE = 32
GROUP = 16
TILES = 2

THETA = (HIGH_END + LOW_END) / 2.0
DELTA = (HIGH_END - LOW_END) / 2.0
SIGMA = THETA / DELTA


def schedule():
    rho = 1.0 / SIGMA
    steps = []
    for _ in range(SWEEPS - 1):
        rho_new = 1.0 / (2.0 * SIGMA - rho)
        steps.append((rho_new * rho, 2.0 * rho_new / DELTA))
        rho = rho_new
    return steps + [(0.0, 0.0)]


def split(value):
    high = value.astype(jnp.bfloat16).astype(jnp.float32)
    return (high, value - high)


def pick(row, index):
    table = jnp.broadcast_to(row, index.shape)
    return jnp.take_along_axis(table, index, axis=1, mode="promise_in_bounds")


def spread(tiles, lane, local):
    first, at = divmod(local * CAP, LANES)
    out = None
    for c, row in enumerate(tiles):
        piece = pltpu.roll(row[first], (c * SPACE - at) % LANES, axis=1)
        left = LANES - at
        if left < CAP:
            rest = pltpu.roll(row[first + 1], (c * SPACE + left) % LANES, axis=1)
            piece = jnp.where(lane < c * SPACE + left, piece, rest)
        out = piece if c == 0 else jnp.where(lane < c * SPACE, out, piece)
    return out


def kernel(
    sizes, force_in, inv_diag_in, k_ref_in, coefs_in, conn_in, felem_in, weights_in, counts,
    celem_in, smoothed, load,
    force, inv_diag, k_ref, coefs, conn, felem, weights, celem,
    direction, resid, scale, total, part, local, onehot, slot_node, values, contrib,
    sent, selector, arrived, stacked, snd, rcv,
    snd_sem, rcv_sem, out_sem, in_sem, own_sem, load_sem,
):
    fine, coarse = sizes
    devices = fine * coarse
    me = lax.axis_index("fine") * coarse + lax.axis_index("coarse")
    nodes = force.shape[1]
    owned = nodes // ROW
    edge = BAND // ROW
    rows = owned + 2 * edge
    stride = total.shape[0] // 3
    elems = conn.shape[1]
    slots = felem.shape[1]
    window = 2 * edge

    half = snd.shape[2] // 2

    def put_edge(phase, d, to, value):
        count = value.shape[0]
        snd[phase, d, to : to + count, :] = value[:, :LANES]
        snd[phase, d, half + to : half + to + count, :] = value[:, LANES:]

    def get_edge(phase, d, to, count):
        return jnp.concatenate(
            [rcv[phase, d, at : at + count, :] for at in (to, half + to)], axis=1
        )

    def place(index):
        return (index // coarse, lax.rem(index, coarse))

    pairs = [
        (force_in, force), (inv_diag_in, inv_diag), (conn_in, conn), (felem_in, felem.at[0]),
        (celem_in, celem), (k_ref_in, k_ref), (coefs_in, coefs.at[0]), (weights_in, weights),
    ]
    loads = [pltpu.make_async_copy(a, b, load_sem.at[n]) for n, (a, b) in enumerate(pairs)]
    for copy in loads:
        copy.start()

    barrier = pltpu.get_barrier_semaphore()

    @pl.loop(1, devices)
    def _(step):
        pl.semaphore_signal(
            barrier, inc=1, device_id=place(lax.rem(me + step, devices)),
            device_id_type=pl.DeviceIdType.MESH,
        )

    resid[...] = jnp.zeros_like(resid)
    scale[...] = jnp.zeros_like(scale)
    loads[0].wait()
    loads[1].wait()
    for c in range(3):
        for h in range(owned):
            at = c * stride + edge + h
            resid[at : at + 1, :] = force[c : c + 1, h * ROW : (h + 1) * ROW]
            scale[at : at + 1, :] = inv_diag[c : c + 1, h * ROW : (h + 1) * ROW]
    for d, begin in enumerate((edge, owned)):
        for a, field in enumerate((resid, scale)):
            for c in range(3):
                at = c * stride + begin
                to = (a * 3 + c) * edge
                put_edge(0, d, to, field[at : at + edge, :])

    for copy in loads[2:5]:
        copy.wait()

    @pl.loop(0, slots // LANES, unroll=2)
    def _(tile):
        at = pl.multiple_of(tile * LANES, LANES)
        element = jnp.broadcast_to(felem[:, pl.ds(at, LANES)], (8, LANES))
        low = jnp.bitwise_and(element, LANES - 1)
        high = lax.shift_right_logical(element, 7)
        found = jnp.zeros((8, LANES), jnp.int32)
        for t in range(elems // LANES):
            got = jnp.take_along_axis(
                conn[:, t * LANES : (t + 1) * LANES], low, axis=1, mode="promise_in_bounds"
            )
            found = jnp.where(high == t, got, found)
        slot_node[:, pl.ds(at, LANES)] = found

    lane = lax.broadcasted_iota(jnp.int32, (8, LANES), 1)
    coarse_iota = lax.broadcasted_iota(jnp.int32, (CE_DEV, LANES), 0)
    group_tiles = GROUP * CAP // LANES

    @pl.loop(0, devices // GROUP)
    def _(group):
        base = group * (GROUP * CAP)
        ids = [
            jnp.broadcast_to(
                celem[:, pl.ds(pl.multiple_of(base + t * LANES, LANES), LANES)], (8, LANES)
            )
            for t in range(group_tiles)
        ]
        for o in range(GROUP):
            owner = spread([ids, ids, ids], lane, o)
            hit = coarse_iota == owner[0:1, :]
            at = pl.multiple_of((group * GROUP + o) * LANES, LANES)
            selector[:, pl.ds(at, LANES)] = jnp.where(hit, 1.0, 0.0).astype(jnp.bfloat16)

    pl.semaphore_wait(barrier, devices - 1)

    lower, upper = (place(lax.rem(me + devices - 1, devices)), place(lax.rem(me + 1, devices)))

    def edge_copy(phase, d, target):
        return pltpu.make_async_remote_copy(
            src_ref=snd.at[phase, d],
            dst_ref=rcv.at[phase, d],
            send_sem=snd_sem.at[phase, d],
            recv_sem=rcv_sem.at[phase, d],
            device_id=target,
            device_id_type=pl.DeviceIdType.MESH,
        )

    def edge_start(phase):
        down, up = edge_copy(phase, 0, lower), edge_copy(phase, 1, upper)

        @pl.when(me > 0)
        def _():
            down.start()

        @pl.when(me < devices - 1)
        def _():
            up.start()

    def edge_wait(phase):
        down, up = edge_copy(phase, 0, lower), edge_copy(phase, 1, upper)

        @pl.when(me > 0)
        def _():
            up.wait_recv()
            down.wait_send()

        @pl.when(me < devices - 1)
        def _():
            down.wait_recv()
            up.wait_send()

    edge_start(0)

    @pl.loop(0, 8)
    def _(j):
        low = jnp.bitwise_and(conn[pl.ds(j, 1), :], ROW - 1)
        hit = lax.broadcasted_iota(jnp.int32, (ROW, elems), 0) == low
        onehot[j] = jnp.where(hit, 1.0, 0.0).astype(jnp.bfloat16)

    for copy in loads[5:]:
        copy.wait()

    def fill_edges():
        @pl.when(me > 0)
        def _():
            for a, field in enumerate((resid, scale)):
                for c in range(3):
                    at, to = (c * stride, (a * 3 + c) * edge)
                    field[at : at + edge, :] = get_edge(0, 1, to, edge)

        @pl.when(me < devices - 1)
        def _():
            for a, field in enumerate((resid, scale)):
                for c in range(3):
                    at, to = (c * stride + edge + owned, (a * 3 + c) * edge)
                    field[at : at + edge, :] = get_edge(0, 0, to, edge)

        direction[...] = scale[...] * resid[...] / THETA

    def add_edges(phase, add):
        def from_side(d, begin):
            for c in range(3):
                at = slice(c * stride + begin, c * stride + begin + window)
                theirs = get_edge(phase, d, c * window, window)
                resid[at, :] -= theirs
                direction[at, :] -= add * scale[at, :] * theirs

        def clear(begin):
            for c in range(3):
                at = c * stride + begin
                resid[at : at + edge, :] = jnp.zeros((edge, ROW), jnp.float32)

        @pl.when(me > 0)
        def _():
            from_side(1, 0)

        @pl.when(me == 0)
        def _():
            clear(0)

        @pl.when(me < devices - 1)
        def _():
            from_side(0, owned)

        @pl.when(me == devices - 1)
        def _():
            clear(edge + owned)

    direction[...] = scale[...] * resid[...] / THETA
    total[...] = jnp.zeros_like(total)

    per_row = ROW // LANES
    inner = range(window * per_row, owned * per_row)
    outer = [h for h in range(rows * per_row) if h not in inner]

    def gather(field, index, hs, out):
        low = [jnp.bitwise_and(i, LANES - 1) for i in index]
        high = [lax.shift_right_logical(i, 7) for i in index]
        for h in hs:
            at, side = divmod(h, per_row)
            here = [i == h for i in high]
            for c in range(3):
                r = c * stride + at
                row = field[r : r + 1, side * LANES : (side + 1) * LANES]
                for t in range(len(index)):
                    out[c][t] = jnp.where(here[t], pick(row, low[t]), out[c][t])
        return out

    def gather_local(hs, first):
        @pl.loop(0, elems // (LANES * TILES))
        def _(chunk):
            starts = [pl.multiple_of((chunk * TILES + t) * LANES, LANES) for t in range(TILES)]
            index = [conn[:, pl.ds(s, LANES)] for s in starts]
            out = [
                [
                    jnp.zeros((8, LANES), jnp.float32)
                    if first
                    else local[c * 8 : (c + 1) * 8, pl.ds(starts[t], LANES)]
                    for t in range(TILES)
                ]
                for c in range(3)
            ]
            got = gather(direction, index, hs, out)
            for c in range(3):
                for t in range(TILES):
                    local[c * 8 : (c + 1) * 8, pl.ds(starts[t], LANES)] = got[c][t]

    row_iota = lax.broadcasted_iota(jnp.int32, (stride, elems), 0)
    steps = schedule()

    @pl.loop(0, SWEEPS)
    def _(sweep):
        gather_local(inner, True)
        edge_wait(sweep)

        @pl.when(sweep == 0)
        def _():
            fill_edges()

        @pl.when(sweep > 0)
        def _():
            add_edges(sweep, jnp.where(sweep == 1, steps[0][1], steps[1][1]))

        total[...] += direction[...]
        gather_local(outer, False)

        product = (
            jnp.dot(
                k_ref[...], local[...], precision=lax.Precision.HIGHEST,
                preferred_element_type=jnp.float32,
            )
            * coefs[...]
        )
        local[...] = product
        part[...] = jnp.zeros_like(part)

        @pl.loop(0, 8, unroll=True)
        def _(j):
            high = lax.shift_right_logical(conn[pl.ds(j, 1), :], 8)
            hit = row_iota == high
            halves = [split(local[pl.ds(c * 8 + j, 1), :]) for c in range(3)]
            left = jnp.concatenate(
                [jnp.where(hit, halves[c][s], 0.0) for s in range(2) for c in range(3)], axis=0
            ).astype(jnp.bfloat16)
            part[...] += lax.dot_general(
                left, onehot[j], (((1,), (1,)), ((), ())), preferred_element_type=jnp.float32
            )

        both = part[: 3 * stride, :] + part[3 * stride :, :]
        part[: 3 * stride, :] = both
        for d, begin in enumerate((0, owned)):
            for c in range(3):
                at = c * stride + begin
                put_edge(sweep + 1, d, c * window, part[at : at + window, :])
        edge_start(sweep + 1)
        new = resid[...] - part[: 3 * stride, :]
        resid[...] = new
        keep = jnp.where(sweep == 0, steps[0][0], steps[1][0])
        add = jnp.where(sweep == 0, steps[0][1], steps[1][1])
        direction[...] = keep * direction[...] + add * scale[...] * new

    @pl.loop(0, slots // LANES, unroll=2)
    def _(tile):
        at = pl.multiple_of(tile * LANES, LANES)
        begun = [[jnp.zeros((8, LANES), jnp.float32)] for _ in range(3)]
        got = gather(resid, [slot_node[:, pl.ds(at, LANES)]], inner, begun)
        for c in range(3):
            contrib[c * 8 : (c + 1) * 8, pl.ds(at, LANES)] = got[c][0]

    edge_wait(SWEEPS)
    add_edges(SWEEPS, 0.0)

    @pl.loop(0, slots // LANES, unroll=2)
    def _(tile):
        at = pl.multiple_of(tile * LANES, LANES)
        begun = [[contrib[c * 8 : (c + 1) * 8, pl.ds(at, LANES)]] for c in range(3)]
        got = gather(resid, [slot_node[:, pl.ds(at, LANES)]], outer, begun)
        for c in range(3):
            values[c * 8 : (c + 1) * 8, :] = got[c][0]
        for c in range(3):
            acc = jnp.zeros((8, LANES), jnp.float32)
            for j in range(8):
                acc = acc + weights[:, j, pl.ds(at, LANES)] * values[c * 8 + j : c * 8 + j + 1, :]
            contrib[c * 8 : (c + 1) * 8, pl.ds(at, LANES)] = acc

    lane_slot = jnp.bitwise_and(lane, SPACE - 1)

    @pl.loop(0, devices // GROUP)
    def _(group):
        base = group * (GROUP * CAP)
        tiles = [
            [
                contrib[
                    c * 8 : (c + 1) * 8,
                    pl.ds(pl.multiple_of(base + t * LANES, LANES), LANES),
                ]
                for t in range(group_tiles)
            ]
            for c in range(3)
        ]
        for o in range(GROUP):
            owner = group * GROUP + o
            live = (lane_slot < counts[0, owner]) & (lane < 3 * SPACE)
            sent[owner] = jnp.where(live, spread(tiles, lane, o), 0.0)

    def slot_copy(target):
        return pltpu.make_async_remote_copy(
            src_ref=sent.at[target],
            dst_ref=arrived.at[me],
            send_sem=out_sem.at[target],
            recv_sem=in_sem.at[me],
            device_id=place(target),
            device_id_type=pl.DeviceIdType.MESH,
        )

    def slot_arrival(source):
        return pltpu.make_async_remote_copy(
            src_ref=sent.at[source],
            dst_ref=arrived.at[source],
            send_sem=out_sem.at[source],
            recv_sem=in_sem.at[source],
            device_id=place(source),
            device_id_type=pl.DeviceIdType.MESH,
        )

    @pl.loop(1, devices)
    def _(step):
        slot_copy(lax.rem(me + step, devices)).start()

    own = pltpu.make_async_copy(sent.at[me], arrived.at[me], own_sem)
    own.start()

    for c in range(3):
        for h in range(owned):
            at = c * stride + edge + h
            smoothed[c : c + 1, h * ROW : (h + 1) * ROW] = total[at : at + 1, :]

    own.wait()

    @pl.loop(1, devices)
    def _(step):
        slot_arrival(lax.rem(me + step, devices)).wait_recv()

    @pl.loop(0, devices)
    def _(source):
        got = arrived[source]
        pieces = [
            split(jnp.where((lane >= c * SPACE) & (lane < (c + 1) * SPACE), got, 0.0))
            for c in range(3)
        ]
        stacked[:, pl.ds(pl.multiple_of(source * LANES, LANES), LANES)] = jnp.concatenate(
            [pieces[c][s] for s in range(2) for c in range(3)], axis=0
        ).astype(jnp.bfloat16)

    sums = lax.dot_general(
        stacked[...], selector[...], (((1,), (1,)), ((), ())), preferred_element_type=jnp.float32
    )
    load[...] = sums[:24, :] + sums[24:, :]

    @pl.loop(1, devices)
    def _(step):
        slot_copy(lax.rem(me + step, devices)).wait_send()


def on_device(sizes, force, inv_diag, k_ref, coefs, conn, felem, weights, counts, celem):
    devices = sizes[0] * sizes[1]
    nodes = force.shape[1]
    elems = conn.shape[1]
    slots = felem.shape[0]
    rows = (nodes + 2 * BAND) // ROW
    stride = -(-rows // 8) * 8
    edge_rows = 6 * BAND // ROW
    field = pltpu.VMEM((3 * stride, ROW), jnp.float32)
    edges = pltpu.VMEM((SWEEPS + 1, 2, edge_rows * ROW // LANES, LANES), jnp.float32)
    vmem = pl.BlockSpec(memory_space=pltpu.VMEM)
    hbm = pl.BlockSpec(memory_space=pltpu.HBM)
    smem = pl.BlockSpec(memory_space=pltpu.SMEM)
    return pl.pallas_call(
        functools.partial(kernel, sizes),
        out_shape=(
            jax.ShapeDtypeStruct((3, nodes), jnp.float32),
            jax.ShapeDtypeStruct((24, CE_DEV), jnp.float32),
        ),
        in_specs=[hbm] * 7 + [smem, hbm],
        out_specs=(vmem, vmem),
        scratch_shapes=[
            pltpu.VMEM((3, nodes), jnp.float32),
            pltpu.VMEM((3, nodes), jnp.float32),
            pltpu.VMEM((24, 24), jnp.float32),
            pltpu.VMEM((1, elems), jnp.float32),
            pltpu.VMEM((8, elems), jnp.int32),
            pltpu.VMEM((1, slots), jnp.int32),
            pltpu.VMEM((8, 8, slots), jnp.float32),
            pltpu.VMEM((1, slots), jnp.int32),
            field,
            field,
            field,
            field,
            pltpu.VMEM((6 * stride, ROW), jnp.float32),
            pltpu.VMEM((24, elems), jnp.float32),
            pltpu.VMEM((8, ROW, elems), jnp.bfloat16),
            pltpu.VMEM((8, slots), jnp.int32),
            pltpu.VMEM((24, LANES), jnp.float32),
            pltpu.VMEM((24, slots), jnp.float32),
            pltpu.VMEM((devices, 8, LANES), jnp.float32),
            pltpu.VMEM((CE_DEV, devices * LANES), jnp.bfloat16),
            pltpu.VMEM((devices, 8, LANES), jnp.float32),
            pltpu.VMEM((48, devices * LANES), jnp.bfloat16),
            edges,
            edges,
            pltpu.SemaphoreType.DMA((SWEEPS + 1, 2)),
            pltpu.SemaphoreType.DMA((SWEEPS + 1, 2)),
            pltpu.SemaphoreType.DMA((devices,)),
            pltpu.SemaphoreType.DMA((devices,)),
            pltpu.SemaphoreType.DMA,
            pltpu.SemaphoreType.DMA((8,)),
        ],
        compiler_params=pltpu.CompilerParams(
            collective_id=0, has_side_effects=True, vmem_limit_bytes=64 * 1024 * 1024
        ),
    )(force, inv_diag, k_ref, coefs, conn, felem, weights, counts, celem)


def solution(mesh):
    both = ("fine", "coarse")
    placed = (
        P(None, both),
        P(None, both),
        P(),
        P(both),
        P(None, both),
        P(both),
        P(None, None, both),
        P(both, None),
        P(both, None),
    )
    sizes = (mesh.shape["fine"], mesh.shape["coarse"])
    return jax.shard_map(
        functools.partial(on_device, sizes),
        mesh=mesh,
        in_specs=placed,
        out_specs=(P(None, both), P(None, both)),
        check_vma=False,
    )
```
